128 devices in a mesh: gx: 4 (over z), gy: 4 (over y), gz: 8 (over x, core).
Axes of the slice: x: 4, y: 4, z: 4, core: 2. Of those that a mesh axis runs over, the one named last changes fastest.
Arguments:
- images: bfloat16 [1024, 197, 384], P(('gx', 'gy', 'gz')), may hold values from -6 to 6
- cotangent: bfloat16 [1024, 197, 384], P(('gx', 'gy', 'gz')), may hold values from -6 to 6
- counts: int32 [128], P(('gx', 'gy', 'gz')), may hold values from 1 to 8, as said below
- ln1_gain: bfloat16 [384], P(('gx', 'gy', 'gz')), may hold values from 0.5 to 1.5
- ln1_bias: bfloat16 [384], P(('gx', 'gy', 'gz')), may hold values from -3 to 3
- w_qkv: bfloat16 [384, 1152], P(('gx', 'gy', 'gz')), may hold values from -0.3125 to 0.3125
- bias_qv: bfloat16 [768], P(('gx', 'gy', 'gz')), may hold values from -3 to 3
- w_out: bfloat16 [384, 384], P(('gx', 'gy', 'gz')), may hold values from -1.75 to 1.75
- b_out: bfloat16 [384], P(('gx', 'gy', 'gz')), may hold values from -3 to 3
- ln2_gain: bfloat16 [384], P(('gx', 'gy', 'gz')), may hold values from 0.5 to 1.5
- ln2_bias: bfloat16 [384], P(('gx', 'gy', 'gz')), may hold values from -3 to 3
- w_up: bfloat16 [384, 1536], P(('gx', 'gy', 'gz')), may hold values from -0.3125 to 0.3125
- b_up: bfloat16 [1536], P(('gx', 'gy', 'gz')), may hold values from -3 to 3
- w_down: bfloat16 [1536, 384], P(('gx', 'gy', 'gz')), may hold values from -0.15625 to 0.15625
- b_down: bfloat16 [384], P(('gx', 'gy', 'gz')), may hold values from -3 to 3
Outputs:
- block_out: float32 [1024, 197, 384], P(('gx', 'gy', 'gz'))
- input_grad: float32 [1024, 197, 384], P(('gx', 'gy', 'gz'))
- grad_ln1_gain: float32 [384], P(('gx', 'gy', 'gz'))
- grad_ln1_bias: float32 [384], P(('gx', 'gy', 'gz'))
- grad_w_qkv: float32 [384, 1152], P(('gx', 'gy', 'gz'))
- grad_bias_qv: float32 [768], P(('gx', 'gy', 'gz'))
- grad_w_out: float32 [384, 384], P(('gx', 'gy', 'gz'))
- grad_b_out: float32 [384], P(('gx', 'gy', 'gz'))
- grad_ln2_gain: float32 [384], P(('gx', 'gy', 'gz'))
- grad_ln2_bias: float32 [384], P(('gx', 'gy', 'gz'))
- grad_w_up: float32 [384, 1536], P(('gx', 'gy', 'gz'))
- grad_b_up: float32 [1536], P(('gx', 'gy', 'gz'))
- grad_w_down: float32 [1536, 384], P(('gx', 'gy', 'gz'))
- grad_b_down: float32 [384], P(('gx', 'gy', 'gz'))
The draws below stay inside these ranges and needn't reach their ends.
Inputs may be any that keep to these rules, and one draw needn't show every extreme that they name: Each device holds 8 image slots, of which the first counts are live; some device is full.
All inputs are finite; a program needn't handle non-finite values.
Results may differ from the reference program's by a relative error of at most 0.015.
Values may be sent and summed in bfloat16 or wider, within the bound.
No kernel may reach another device: no remote copies, remote signals or barrier semaphores. Data moves between devices by JAX's collectives and lax.ppermute only.
A program may use at most 192 MiB of HBM per device.

```python
import jax
import jax.numpy as jnp
from jax import lax

D = 384
FF = 1536
HEADS = 6
TOK = 197
HEAD = 64
CAP = 8
SLOTS = 1024


def draw_counts(key, part):
    groups = SLOTS // CAP
    values = jax.random.randint(key, (groups,), 1, CAP + 1)
    chosen = jax.random.randint(jax.random.fold_in(key, 7), (), 0, groups)
    return jnp.where(jnp.arange(groups) == chosen, CAP, values).astype(jnp.int32)


def steps_of(stream_key, shape, split, low, top_value):
    level, own = 1.0, jax.random.fold_in(stream_key, 6)
    for dim, blocks in split:
        heights = jnp.exp(jax.random.uniform(jax.random.fold_in(own, dim), (blocks,), jnp.float32, low / len(split), top_value / len(split)))
        level = level * jnp.repeat(heights, shape[dim] // blocks).reshape([-1 if axis == dim else 1 for axis in range(len(shape))])
    return level


def bell_draw(own_key, dims, scale, reach, pieces=(), kind=jnp.bfloat16):
    array = scale * jax.random.normal(own_key, dims, jnp.float32)
    if pieces:
        array = array * steps_of(own_key, dims, pieces, -0.22, 0.18)
    return jnp.clip(array, -reach, reach).astype(kind)


def setup_inputs(seed: int = 0) -> dict:
    seeds = jax.random.split(jax.random.key(seed), 16)
    images = bell_draw(seeds[0], (SLOTS, TOK, D), 1.0, 6.0, ((0, 128),))
    cotangent = bell_draw(seeds[1], (SLOTS, TOK, D), 1.0, 6.0, ((0, 128),))
    counts = draw_counts(jax.random.fold_in(seeds[15], 71), 0)
    ln1_gain = jnp.clip(1.0 + 0.1 * jax.random.normal(seeds[3], (D,), jnp.float32), 0.5, 1.5).astype(jnp.bfloat16)
    ln1_bias = bell_draw(seeds[4], (D,), 0.5, 3.0, ((0, 128),))
    w_qkv = bell_draw(seeds[5], (D, 3 * D), D ** -0.5, 0.3125, ((0, 128),))
    bias_qv = bell_draw(seeds[6], (2 * D,), 0.5, 3.0, ((0, 128),))
    w_out = bell_draw(seeds[7], (D, D), (D // 32) ** -0.5, 1.75, ((0, 128),))
    b_out = bell_draw(seeds[8], (D,), 0.5, 3.0, ((0, 128),))
    ln2_gain = jnp.clip(1.0 + 0.1 * jax.random.normal(seeds[9], (D,), jnp.float32), 0.5, 1.5).astype(jnp.bfloat16)
    ln2_bias = bell_draw(seeds[10], (D,), 0.5, 3.0, ((0, 128),))
    w_up = bell_draw(seeds[11], (D, FF), D ** -0.5, 0.3125, ((0, 128),))
    b_up = bell_draw(seeds[12], (FF,), 0.5, 3.0, ((0, 128),))
    w_down = bell_draw(seeds[13], (FF, D), FF ** -0.5, 0.15625, ((0, 128),))
    b_down = bell_draw(seeds[14], (D,), 0.5, 3.0, ((0, 128),))
    return dict(images=images, cotangent=cotangent, counts=counts, ln1_gain=ln1_gain, ln1_bias=ln1_bias, w_qkv=w_qkv, bias_qv=bias_qv, w_out=w_out, b_out=b_out, ln2_gain=ln2_gain, ln2_bias=ln2_bias, w_up=w_up, b_up=b_up, w_down=w_down, b_down=b_down)


epsilon = 1e-06
score_scale = 0.125
root_half = 0.7071067811865476
inv_root_two_pi = 0.3989422804014327

def norm_forward(values, gain, shift):
    center = values - lax.optimization_barrier(jnp.mean(values, -1, keepdims=True))
    inverse = lax.rsqrt(lax.optimization_barrier(jnp.mean(center * center, -1, keepdims=True)) + epsilon)
    normed = center * inverse
    return (normed, inverse, normed * gain.astype(jnp.float32) + shift.astype(jnp.float32))

def norm_backward(upstream, normed, inverse, gain):
    scaled = upstream * gain.astype(jnp.float32)
    return inverse * (scaled - lax.optimization_barrier(jnp.mean(scaled, -1, keepdims=True)) - normed * lax.optimization_barrier(jnp.mean(scaled * normed, -1, keepdims=True)))

def gelu_parts(before):
    cdf_value = 0.5 * (1.0 + lax.erf(before * root_half))
    return (before * cdf_value, cdf_value + before * jnp.exp(-0.5 * before * before) * inv_root_two_pi)

def product(left, right):
    return jnp.dot(left, right, preferred_element_type=jnp.float32)

def block_pass(block_in, block_cot, live, params):
    ln1_gain, ln1_bias, w_qkv, bias_qv, w_out, b_out, ln2_gain, ln2_bias, w_up, b_up, w_down, b_down = params
    images_here, tokens_here, width = block_in.shape
    rows = images_here * tokens_here
    inputs = block_in.astype(jnp.float32).reshape(rows, width)
    normed1, inverse1, first = norm_forward(inputs, ln1_gain, ln1_bias)
    first_b = first.astype(jnp.bfloat16)
    joined = product(first_b, w_qkv)
    query = ((joined[:, :width] + bias_qv[:width].astype(jnp.float32)) * score_scale).astype(jnp.bfloat16)
    key_rows = joined[:, width:2 * width].astype(jnp.bfloat16)
    value = (joined[:, 2 * width:] + bias_qv[width:].astype(jnp.float32)).astype(jnp.bfloat16)
    shape4 = (images_here, tokens_here, HEADS, HEAD)
    query_f = query.reshape(shape4).astype(jnp.float32)
    key_f = key_rows.reshape(shape4).astype(jnp.float32)
    value_f = value.reshape(shape4).astype(jnp.float32)
    scores = jnp.einsum('bqhe,bkhe->bhqk', query_f, key_f)
    top = lax.optimization_barrier(jnp.max(scores, -1, keepdims=True))
    lse = top + jnp.log(lax.optimization_barrier(jnp.sum(jnp.exp(scores - top), -1, keepdims=True)))
    probs = jnp.exp(scores - lse)
    probs_b = probs.astype(jnp.bfloat16)
    attended = jnp.einsum('bhqk,bkhe->bqhe', probs_b.astype(jnp.float32), value_f).reshape(rows, width).astype(jnp.bfloat16)
    mixed = inputs + product(attended, w_out) + b_out.astype(jnp.float32)
    normed2, inverse2, second = norm_forward(mixed, ln2_gain, ln2_bias)
    second_b = second.astype(jnp.bfloat16)
    before = product(second_b, w_up) + b_up.astype(jnp.float32)
    gelu_value, slope = gelu_parts(before)
    active = gelu_value.astype(jnp.bfloat16)
    output = mixed + product(active, w_down) + b_down.astype(jnp.float32)
    upstream = (block_cot.astype(jnp.float32) * live[:, None, None]).reshape(rows, width)
    grad_b_down = lax.optimization_barrier(jnp.sum(upstream, 0))
    upstream_b = upstream.astype(jnp.bfloat16)
    grad_w_down = product(active.T, upstream_b)
    d_before = product(upstream_b, w_down.T) * slope
    grad_b_up = lax.optimization_barrier(jnp.sum(d_before, 0))
    d_before_b = d_before.astype(jnp.bfloat16)
    grad_w_up = product(second_b.T, d_before_b)
    d_second = product(d_before_b, w_up.T)
    grad_ln2_gain = lax.optimization_barrier(jnp.sum(d_second * normed2, 0))
    grad_ln2_bias = lax.optimization_barrier(jnp.sum(d_second, 0))
    d_mixed = upstream + norm_backward(d_second, normed2, inverse2, ln2_gain)
    grad_b_out = lax.optimization_barrier(jnp.sum(d_mixed, 0))
    d_mixed_b = d_mixed.astype(jnp.bfloat16)
    grad_w_out = product(attended.T, d_mixed_b)
    d_attended = product(d_mixed_b, w_out.T).astype(jnp.bfloat16)
    d_att_f = d_attended.reshape(shape4).astype(jnp.float32)
    att_f = attended.reshape(shape4).astype(jnp.float32)
    delta = jnp.einsum('bqhe,bqhe->bhq', d_att_f, att_f)[..., None]
    d_probs = jnp.einsum('bqhe,bkhe->bhqk', d_att_f, value_f)
    d_scores = (probs * (d_probs - delta)).astype(jnp.bfloat16).astype(jnp.float32)
    d_query = jnp.einsum('bhqk,bkhe->bqhe', d_scores, key_f).reshape(rows, width) * score_scale
    d_key = jnp.einsum('bhqk,bqhe->bkhe', d_scores, query_f).reshape(rows, width)
    d_value = jnp.einsum('bhqk,bqhe->bkhe', probs_b.astype(jnp.float32), d_att_f).reshape(rows, width)
    grad_bias_qv = jnp.concatenate([lax.optimization_barrier(jnp.sum(d_query, 0)), lax.optimization_barrier(jnp.sum(d_value, 0))])
    d_joined_b = jnp.concatenate([d_query, d_key, d_value], -1).astype(jnp.bfloat16)
    grad_w_qkv = product(first_b.T, d_joined_b)
    d_first = product(d_joined_b, w_qkv.T)
    grad_ln1_gain = lax.optimization_barrier(jnp.sum(d_first * normed1, 0))
    grad_ln1_bias = lax.optimization_barrier(jnp.sum(d_first, 0))
    d_inputs = d_mixed + norm_backward(d_first, normed1, inverse1, ln1_gain)
    grads = (grad_ln1_gain, grad_ln1_bias, grad_w_qkv, grad_bias_qv, grad_w_out, grad_b_out, grad_ln2_gain, grad_ln2_bias, grad_w_up, grad_b_up, grad_w_down, grad_b_down)
    return (output.reshape(block_in.shape), d_inputs.reshape(block_in.shape), grads)

def reference(images, cotangent, counts, ln1_gain, ln1_bias, w_qkv, bias_qv, w_out, b_out, ln2_gain, ln2_bias, w_up, b_up, w_down, b_down):
    params = (ln1_gain, ln1_bias, w_qkv, bias_qv, w_out, b_out, ln2_gain, ln2_bias, w_up, b_up, w_down, b_down)
    groups = images.shape[0] // CAP
    blocks_in = images.reshape(groups, CAP, TOK, D)
    blocks_cot = cotangent.reshape(groups, CAP, TOK, D)
    slot_index = jnp.arange(CAP, dtype=jnp.int32)

    def step(totals, item):
        block_in, block_cot, count = item
        live = (slot_index < count).astype(jnp.float32)
        output, d_inputs, grads = block_pass(block_in, block_cot, live, params)
        return (tuple((total + grad for total, grad in zip(totals, grads))), (output, d_inputs))
    zeros = tuple((jnp.zeros(param.shape, jnp.float32) for param in params))
    totals, (outputs, d_inputs) = lax.scan(step, zeros, (blocks_in, blocks_cot, counts.astype(jnp.int32)))
    return (outputs.reshape(images.shape), d_inputs.reshape(images.shape), totals[0], totals[1], totals[2], totals[3], totals[4], totals[5], totals[6], totals[7], totals[8], totals[9], totals[10], totals[11])
```

```python
import jax
import jax.numpy as jnp
from jax import lax
from jax.experimental import pallas as pl
from jax.experimental.pallas import tpu as pltpu
from jax.sharding import Mesh
from jax.sharding import PartitionSpec as P

HEADS = 6
HEAD = 64
PAIRS = HEADS // 2
CHIPS = ("gx", "gy", "gz_0")
ROW = ("gz_0", "gz_1")
EVERY = ("gx", "gy", "gz_0", "gz_1")
f32 = jnp.float32
bf16 = jnp.bfloat16

epsilon = 1e-06
score_scale = 0.125
root_half = 0.7071067811865476
inv_root_two_pi = 0.3989422804014327


def dot(left, right):
    return jnp.dot(left, right, preferred_element_type=f32)


def dot_nt(left, right):
    return lax.dot_general(left, right, (((1,), (1,)), ((), ())), preferred_element_type=f32)


def dot_tn(left, right):
    return lax.dot_general(left, right, (((0,), (0,)), ((), ())), preferred_element_type=f32)


def norm_stats(values):
    center = values - jnp.mean(values, -1, keepdims=True)
    inverse = lax.rsqrt(jnp.mean(center * center, -1, keepdims=True) + epsilon)
    return center * inverse, inverse


def norm_backward(upstream, normed, inverse, gain):
    scaled = upstream * gain
    return inverse * (
        scaled
        - jnp.mean(scaled, -1, keepdims=True)
        - normed * jnp.mean(scaled * normed, -1, keepdims=True)
    )


def column_sum(values):
    return jnp.sum(values, 0, keepdims=True)


def attention_forward(img, w, vec, x2_out, qkv_out, att_out, probs_out):
    width = img.shape[-1]
    inputs = img[0].astype(f32)
    normed, _ = norm_stats(inputs)
    first = (normed * vec[0:1, :] + vec[1:2, :]).astype(bf16)
    joined = dot(first, w[:, : 3 * width])
    query = ((joined[:, :width] + vec[6:7, :]) * score_scale).astype(bf16)
    keys = joined[:, width : 2 * width].astype(bf16)
    value = (joined[:, 2 * width :] + vec[7:8, :]).astype(bf16)
    qkv_out[0, :, :width] = query
    qkv_out[0, :, width : 2 * width] = keys
    qkv_out[0, :, 2 * width :] = value
    lane = lax.broadcasted_iota(jnp.int32, (inputs.shape[0], 2 * HEAD), 1)
    low = lane < HEAD
    zero = jnp.zeros((), bf16)
    joined_heads = []
    for p in range(PAIRS):
        cols = slice(2 * HEAD * p, 2 * HEAD * (p + 1))
        q, k, v = query[:, cols], keys[:, cols], value[:, cols]
        outs = []
        for a in range(2):
            masked = jnp.where(low if a == 0 else jnp.logical_not(low), q, zero)
            scores = dot_nt(masked, k)
            top = jnp.max(scores, -1, keepdims=True)
            raised = jnp.exp(scores - top)
            probs = (raised * (1.0 / jnp.sum(raised, -1, keepdims=True))).astype(bf16)
            probs_out[0, 2 * p + a] = probs
            outs.append(dot(probs, v))
        joined_heads.append(jnp.where(low, outs[0], outs[1]).astype(bf16))
    attended = jnp.concatenate(joined_heads, axis=-1)
    att_out[0] = attended
    x2_out[0] = inputs + dot(attended, w[:, 3 * width : 4 * width]) + vec[2:3, :]


def feed_forward(counts, x2, cot, w, vec, out, dx2_out, grad_out, vec_out, gup, gdown, vacc):
    i = pl.program_id(0)
    width = x2.shape[-1]
    hidden = 4 * width

    @pl.when(i == 0)
    def _():
        gup[...] = jnp.zeros_like(gup)
        gdown[...] = jnp.zeros_like(gdown)
        vacc[...] = jnp.zeros_like(vacc)

    mixed = x2[0]
    normed, inverse = norm_stats(mixed)
    gain = vec[3:4, :]
    second = (normed * gain + vec[4:5, :]).astype(bf16)
    live = (i < counts[0]).astype(f32)
    upstream = cot[0].astype(f32) * live
    upstream_b = upstream.astype(bf16)
    total = mixed + vec[5:6, :]
    d_second = jnp.zeros_like(mixed)
    for s in range(4):
        cols = slice(s * width, (s + 1) * width)
        down = slice(hidden + s * width, hidden + (s + 1) * width)
        before = dot(second, w[:, cols]) + vec[8 + s : 9 + s, :]
        cdf = 0.5 * (1.0 + lax.erf(before * root_half))
        active = (before * cdf).astype(bf16)
        slope = cdf + before * jnp.exp(-0.5 * before * before) * inv_root_two_pi
        total = total + dot(active, w[:, down])
        d_before = dot_nt(upstream_b, w[:, down]) * slope
        vacc[8 + s : 9 + s, :] += column_sum(d_before)
        d_before_b = d_before.astype(bf16)
        gdown[:, cols] += dot_tn(upstream_b, active)
        gup[:, cols] += dot_tn(second, d_before_b)
        d_second = d_second + dot_nt(d_before_b, w[:, cols])
    out[0] = total
    d_mixed = upstream + norm_backward(d_second, normed, inverse, gain)
    dx2_out[0] = d_mixed
    vacc[2:3, :] += column_sum(d_mixed)
    vacc[3:4, :] += column_sum(d_second * normed)
    vacc[4:5, :] += column_sum(d_second)
    vacc[5:6, :] += column_sum(upstream)

    @pl.when(i == pl.num_programs(0) - 1)
    def _():
        grad_out[:, :hidden] = gup[...].astype(bf16)
        for s in range(4):
            grad_out[:, hidden + s * width : hidden + (s + 1) * width] = jnp.transpose(
                gdown[:, s * width : (s + 1) * width]
            ).astype(bf16)
        vec_out[...] = vacc[...]


def attention_backward(img, dx2, qkv, att, probs, w, vec, vec_in, dimg, grad_out, gqkv, gout, vacc):
    i = pl.program_id(0)
    width = img.shape[-1]

    @pl.when(i == 0)
    def _():
        gqkv[...] = jnp.zeros_like(gqkv)
        gout[...] = jnp.zeros_like(gout)
        vacc[...] = jnp.zeros_like(vacc)
        vacc[0:16, :] = vec_in[...]

    gain = vec[0:1, :]
    normed, inverse = norm_stats(img[0].astype(f32))
    first = (normed * gain + vec[1:2, :]).astype(bf16)
    d_mixed = dx2[0]
    d_mixed_b = d_mixed.astype(bf16)
    attended = att[0]
    gout[...] += dot_tn(attended, d_mixed_b)
    d_att = dot_nt(d_mixed_b, w[:, 3 * width : 4 * width]).astype(bf16)
    products = d_att.astype(f32) * attended.astype(f32)
    lane = lax.broadcasted_iota(jnp.int32, (normed.shape[0], 2 * HEAD), 1)
    low = lane < HEAD
    zero = jnp.zeros((), bf16)
    d_q, d_k, d_v = [], [], []
    for p in range(PAIRS):
        cols = slice(2 * HEAD * p, 2 * HEAD * (p + 1))
        q = qkv[0, :, cols]
        k = qkv[0, :, width + 2 * HEAD * p : width + 2 * HEAD * (p + 1)]
        v = qkv[0, :, 2 * width + 2 * HEAD * p : 2 * width + 2 * HEAD * (p + 1)]
        da = d_att[:, cols]
        both = products[:, cols]
        parts = []
        for a in range(2):
            mine = low if a == 0 else jnp.logical_not(low)
            delta = jnp.sum(jnp.where(mine, both, 0.0), -1, keepdims=True)
            pb = probs[0, 2 * p + a]
            d_probs = dot_nt(jnp.where(mine, da, zero), v)
            d_scores = (pb.astype(f32) * (d_probs - delta)).astype(bf16)
            parts.append((dot(d_scores, k), dot_tn(d_scores, q), dot_tn(pb, da)))
        d_q.append(jnp.where(low, parts[0][0], parts[1][0]) * score_scale)
        d_k.append(jnp.where(low, parts[0][1], parts[1][1]))
        d_v.append(jnp.where(low, parts[0][2], parts[1][2]))
    d_query = jnp.concatenate(d_q, axis=-1)
    d_value = jnp.concatenate(d_v, axis=-1)
    d_joined = jnp.concatenate([d_query, jnp.concatenate(d_k, axis=-1), d_value], axis=-1).astype(bf16)
    gqkv[...] += dot_tn(first, d_joined)
    d_first = dot_nt(d_joined, w[:, : 3 * width])
    dimg[0] = d_mixed + norm_backward(d_first, normed, inverse, gain)
    vacc[0:1, :] += column_sum(d_first * normed)
    vacc[1:2, :] += column_sum(d_first)
    vacc[6:7, :] += column_sum(d_query)
    vacc[7:8, :] += column_sum(d_value)

    @pl.when(i == pl.num_programs(0) - 1)
    def _():
        grad_out[:, : 3 * width] = gqkv[...].astype(bf16)
        grad_out[:, 3 * width : 4 * width] = gout[...].astype(bf16)
        source = lax.broadcasted_iota(jnp.int32, (width, width), 0)
        target = lax.broadcasted_iota(jnp.int32, (width, width), 1)
        pair = vacc[0:8, :].astype(bf16)
        mixed = []
        for j in range(2):
            take_q = (source == 2 * target + j).astype(f32).astype(bf16)
            take_v = (source + width == 2 * target + j).astype(f32).astype(bf16)
            mixed.append(dot(pair, take_q)[6:7, :] + dot(pair, take_v)[7:8, :])
        vacc[6:7, :] = mixed[0]
        vacc[7:8, :] = mixed[1]
        grad_out[:, 4 * width : 4 * width + 128] = jnp.transpose(vacc[...]).astype(bf16)
        rest = grad_out.shape[1] - 4 * width - 128
        grad_out[:, 4 * width + 128 :] = jnp.zeros((width, rest), bf16)


def per_image(*dims):
    return pl.BlockSpec((1, *dims), lambda i: (i,) + (0,) * len(dims))


def fixed(*dims):
    return pl.BlockSpec(dims, lambda i: (0,) * len(dims), pipeline_mode=pl.Buffered(1))


def kept(*dims):
    return pl.BlockSpec(dims, lambda i: (0,) * len(dims))


SERIAL = pltpu.CompilerParams(dimension_semantics=("arbitrary",), vmem_limit_bytes=60 << 20)


def gather(shard):
    rows, cols = shard.shape
    near, n = 8, cols // 8
    pieces = jnp.transpose(shard.reshape(rows, near, n), (1, 0, 2))
    pieces = lax.all_to_all(pieces, ROW, 0, 0, tiled=True).reshape(near * rows, n)
    spread = jnp.broadcast_to(pieces[None], (64, near * rows, n))
    mine = lax.all_to_all(spread, CHIPS, 0, 0, tiled=True)
    other = lax.ppermute(mine, "gz_1", [(0, 1), (1, 0)])
    first = lax.axis_index("gz_1") == 0
    pair = jnp.stack([jnp.where(first, mine, other), jnp.where(first, other, mine)])
    pair = pair.reshape(2, 16, 4, near * rows, n)
    return jnp.transpose(pair, (1, 3, 2, 0, 4)).reshape(16 * near * rows, cols)


def reduce(grad):
    rows, cols = grad.shape
    n, block = cols // 8, rows // 16
    parts = jnp.transpose(grad.reshape(16, block, 4, 2, n), (3, 0, 2, 1, 4))
    first = lax.axis_index("gz_1") == 0
    mine = jnp.where(first, parts[0], parts[1])
    theirs = lax.ppermute(jnp.where(first, parts[1], parts[0]), "gz_1", [(0, 1), (1, 0)])
    half = (mine.astype(f32) + theirs.astype(f32)).astype(bf16).reshape(64, block, n)
    half = lax.all_to_all(half, CHIPS, 0, 0, tiled=True)
    own = jnp.sum(half.astype(f32), 0).reshape(8, block // 8, n)
    own = lax.all_to_all(own, ROW, 0, 0, tiled=True)
    return jnp.transpose(own, (1, 0, 2)).reshape(block // 8, cols)


def per_device(
    images,
    cotangent,
    counts,
    ln1_gain,
    ln1_bias,
    w_qkv,
    bias_qv,
    w_out,
    b_out,
    ln2_gain,
    ln2_bias,
    w_up,
    b_up,
    w_down,
    b_down,
):
    slots, tokens, width = images.shape
    rows = w_qkv.shape[0]
    hidden = 4 * width
    vectors = jnp.concatenate(
        [
            jnp.stack([ln1_gain, ln1_bias, b_out, ln2_gain, ln2_bias, b_down], axis=1),
            bias_qv.reshape(rows, 2),
            b_up.reshape(rows, 4),
        ],
        axis=1,
    )
    spare = 2048 - 4 * width - vectors.shape[1]
    shard_one = jnp.concatenate([w_qkv, w_out, vectors, jnp.zeros((rows, spare), bf16)], axis=1)
    up_turned = jnp.transpose(w_up.reshape(rows, width, 4), (0, 2, 1)).reshape(rows, hidden)
    shard_two = jnp.concatenate([up_turned, w_down.reshape(rows, hidden)], axis=1)
    w_one = gather(shard_one)
    w_two = gather(shard_two)
    turned = jnp.transpose(w_one[:, hidden : hidden + 16].astype(f32))
    biases = w_one[:, hidden + 6 : hidden + 8].astype(f32).reshape(2, width)
    vec = jnp.concatenate([turned[:6], biases, turned[8:]], axis=0)

    x2, qkv, attended, probs = pl.pallas_call(
        attention_forward,
        grid=(slots,),
        in_specs=[per_image(tokens, width), fixed(width, 2048), fixed(16, width)],
        out_specs=[
            per_image(tokens, width),
            per_image(tokens, 3 * width),
            per_image(tokens, width),
            per_image(HEADS, tokens, tokens),
        ],
        out_shape=[
            jax.ShapeDtypeStruct((slots, tokens, width), f32),
            jax.ShapeDtypeStruct((slots, tokens, 3 * width), bf16),
            jax.ShapeDtypeStruct((slots, tokens, width), bf16),
            jax.ShapeDtypeStruct((slots, HEADS, tokens, tokens), bf16),
        ],
        compiler_params=SERIAL,
        name="attention_forward",
    )(images, w_one, vec)

    output, dx2, grad_two, vec_two = pl.pallas_call(
        feed_forward,
        grid=(slots,),
        in_specs=[
            pl.BlockSpec(memory_space=pltpu.SMEM),
            per_image(tokens, width),
            per_image(tokens, width),
            fixed(width, 2 * hidden),
            fixed(16, width),
        ],
        out_specs=[
            per_image(tokens, width),
            per_image(tokens, width),
            kept(width, 2 * hidden),
            kept(16, width),
        ],
        out_shape=[
            jax.ShapeDtypeStruct((slots, tokens, width), f32),
            jax.ShapeDtypeStruct((slots, tokens, width), f32),
            jax.ShapeDtypeStruct((width, 2 * hidden), bf16),
            jax.ShapeDtypeStruct((16, width), f32),
        ],
        scratch_shapes=[
            pltpu.VMEM((width, hidden), f32),
            pltpu.VMEM((width, hidden), f32),
            pltpu.VMEM((16, width), f32),
        ],
        compiler_params=SERIAL,
        name="feed_forward",
    )(counts, x2, cotangent, w_two, vec)

    d_images, grad_one = pl.pallas_call(
        attention_backward,
        grid=(slots,),
        in_specs=[
            per_image(tokens, width),
            per_image(tokens, width),
            per_image(tokens, 3 * width),
            per_image(tokens, width),
            per_image(HEADS, tokens, tokens),
            fixed(width, 2048),
            fixed(16, width),
            fixed(16, width),
        ],
        out_specs=[per_image(tokens, width), kept(width, 2048)],
        out_shape=[
            jax.ShapeDtypeStruct((slots, tokens, width), f32),
            jax.ShapeDtypeStruct((width, 2048), bf16),
        ],
        scratch_shapes=[
            pltpu.VMEM((width, 3 * width), f32),
            pltpu.VMEM((width, width), f32),
            pltpu.VMEM((128, width), f32),
        ],
        compiler_params=SERIAL,
        name="attention_backward",
    )(images, dx2, qkv, attended, probs, w_one, vec, vec_two)

    two = reduce(grad_two)
    one = reduce(grad_one)
    small = one[:, hidden : hidden + 12]
    up = jnp.transpose(two[:, :hidden].reshape(rows, 4, width), (0, 2, 1)).reshape(rows, hidden)
    return (
        output,
        d_images,
        small[:, 0],
        small[:, 1],
        one[:, : 3 * width],
        small[:, 6:8].reshape(-1),
        one[:, 3 * width : hidden],
        small[:, 2],
        small[:, 3],
        small[:, 4],
        up,
        small[:, 8:12].reshape(-1),
        two[:, hidden:].reshape(4 * rows, width),
        small[:, 5],
    )


def solution(mesh):
    torus = Mesh(
        mesh.devices.reshape(mesh.shape["gx"], mesh.shape["gy"], 4, 2), ("gx", "gy", "gz_0", "gz_1")
    )
    whole, flat, table = P(EVERY, None, None), P(EVERY), P(EVERY, None)
    params = (flat, flat, table, flat, table, flat, flat, flat, table, flat, table, flat)
    return jax.shard_map(
        per_device,
        mesh=torus,
        in_specs=(whole, whole, flat, *params),
        out_specs=(whole, whole, *params),
        check_vma=False,
    )
```

```python
import jax
import jax.numpy as jnp
from jax import lax
from jax.experimental import pallas as pl
from jax.experimental.pallas import tpu as pltpu
from jax.sharding import Mesh
from jax.sharding import PartitionSpec as P

HEADS = 6
HEAD = 64
PAIRS = HEADS // 2
CHIPS = ("gx", "gy", "gz_0")
ROW = ("gz_0", "gz_1")
EVERY = ("gx", "gy", "gz_0", "gz_1")
f32 = jnp.float32
bf16 = jnp.bfloat16

epsilon = 1e-06
score_scale = 0.125
root_half = 0.7071067811865476
inv_root_two_pi = 0.3989422804014327


def dot(left, right):
    return jnp.dot(left, right, preferred_element_type=f32)


def dot_nt(left, right):
    return lax.dot_general(left, right, (((1,), (1,)), ((), ())), preferred_element_type=f32)


def dot_tn(left, right):
    return lax.dot_general(left, right, (((0,), (0,)), ((), ())), preferred_element_type=f32)


def norm_stats(values):
    center = values - jnp.mean(values, -1, keepdims=True)
    inverse = lax.rsqrt(jnp.mean(center * center, -1, keepdims=True) + epsilon)
    return center * inverse, inverse


def norm_backward(upstream, normed, inverse, gain):
    scaled = upstream * gain
    return inverse * (
        scaled
        - jnp.mean(scaled, -1, keepdims=True)
        - normed * jnp.mean(scaled * normed, -1, keepdims=True)
    )


def column_sum(values):
    return jnp.sum(values, 0, keepdims=True)


def unpack(low, own, other, put):
    for b in range(16):
        for x in range(4):
            mine, theirs = own[4 * b + x], other[4 * b + x]
            put(b, 2 * x, jnp.where(low, mine, theirs))
            put(b, 2 * x + 1, jnp.where(low, theirs, mine))


def pack(low, take, mine, theirs):
    for b in range(16):
        for x in range(4):
            even, odd = take(b, 2 * x).astype(bf16), take(b, 2 * x + 1).astype(bf16)
            mine[4 * b + x] = jnp.where(low, even, odd)
            theirs[4 * b + x] = jnp.where(low, odd, even)


def attention_forward(side, img, own, other, x2_out, qkv_out, att_out, probs_out, w, vec):
    width = img.shape[-1]
    block, n = own.shape[1:]

    @pl.when(pl.program_id(0) == 0)
    def _():
        tables = []

        def put(b, s, piece):
            if (s + 1) * n <= 4 * width:
                w[b * block : (b + 1) * block, s * n : (s + 1) * n] = piece
            elif s * n == 4 * width:
                tables.append(piece[:, :128].astype(f32))

        unpack(side[0] == 0, own, other, put)
        turned = jnp.transpose(jnp.concatenate(tables, axis=0))[:16, :]
        vec[...] = turned
        source = lax.broadcasted_iota(jnp.int32, (width, width), 0)
        target = lax.broadcasted_iota(jnp.int32, (width, width), 1)
        pair = turned.astype(bf16)
        for k in range(2):
            even = (2 * source == target + k * width).astype(f32).astype(bf16)
            odd = (2 * source + 1 == target + k * width).astype(f32).astype(bf16)
            vec[6 + k : 7 + k, :] = dot(pair, even)[6:7, :] + dot(pair, odd)[7:8, :]

    inputs = img[0].astype(f32)
    normed, _ = norm_stats(inputs)
    first = (normed * vec[0:1, :] + vec[1:2, :]).astype(bf16)
    joined = dot(first, w[:, : 3 * width])
    query = ((joined[:, :width] + vec[6:7, :]) * score_scale).astype(bf16)
    keys = joined[:, width : 2 * width].astype(bf16)
    value = (joined[:, 2 * width :] + vec[7:8, :]).astype(bf16)
    qkv_out[0, :, :width] = query
    qkv_out[0, :, width : 2 * width] = keys
    qkv_out[0, :, 2 * width :] = value
    lane = lax.broadcasted_iota(jnp.int32, (inputs.shape[0], 2 * HEAD), 1)
    low = lane < HEAD
    zero = jnp.zeros((), bf16)
    joined_heads = []
    for p in range(PAIRS):
        cols = slice(2 * HEAD * p, 2 * HEAD * (p + 1))
        q, k, v = query[:, cols], keys[:, cols], value[:, cols]
        outs = []
        for a in range(2):
            masked = jnp.where(low if a == 0 else jnp.logical_not(low), q, zero)
            scores = dot_nt(masked, k)
            top = jnp.max(scores, -1, keepdims=True)
            raised = jnp.exp(scores - top)
            probs = (raised * (1.0 / jnp.sum(raised, -1, keepdims=True))).astype(bf16)
            probs_out[0, 2 * p + a] = probs
            outs.append(dot(probs, v))
        joined_heads.append(jnp.where(low, outs[0], outs[1]).astype(bf16))
    attended = jnp.concatenate(joined_heads, axis=-1)
    att_out[0] = attended
    x2_out[0] = inputs + dot(attended, w[:, 3 * width : 4 * width]) + vec[2:3, :]


def feed_forward(
    side, counts, x2, cot, own, other, vec, out, dx2_out, mine, theirs, vec_out, w, gup, gdown, vacc
):
    i = pl.program_id(0)
    width = x2.shape[-1]
    hidden = 4 * width
    block = own.shape[1]

    @pl.when(i == 0)
    def _():
        def put(b, s, piece):
            w[b * block : (b + 1) * block, s * width : (s + 1) * width] = piece

        unpack(side[0] == 0, own, other, put)
        gup[...] = jnp.zeros_like(gup)
        gdown[...] = jnp.zeros_like(gdown)
        vacc[...] = jnp.zeros_like(vacc)

    mixed = x2[0]
    normed, inverse = norm_stats(mixed)
    gain = vec[3:4, :]
    second = (normed * gain + vec[4:5, :]).astype(bf16)
    live = (i < counts[0]).astype(f32)
    upstream = cot[0].astype(f32) * live
    upstream_b = upstream.astype(bf16)
    total = mixed + vec[5:6, :]
    d_second = jnp.zeros_like(mixed)
    for s in range(4):
        cols = slice(s * width, (s + 1) * width)
        down = slice(hidden + s * width, hidden + (s + 1) * width)
        before = dot(second, w[:, cols]) + vec[8 + s : 9 + s, :]
        cdf = 0.5 * (1.0 + lax.erf(before * root_half))
        active = (before * cdf).astype(bf16)
        slope = cdf + before * jnp.exp(-0.5 * before * before) * inv_root_two_pi
        total = total + dot(active, w[:, down])
        d_before = dot_nt(upstream_b, w[:, down]) * slope
        vacc[8 + s : 9 + s, :] += column_sum(d_before)
        d_before_b = d_before.astype(bf16)
        gdown[:, cols] += dot_tn(upstream_b, active)
        gup[:, cols] += dot_tn(second, d_before_b)
        d_second = d_second + dot_nt(d_before_b, w[:, cols])
    out[0] = total
    d_mixed = upstream + norm_backward(d_second, normed, inverse, gain)
    dx2_out[0] = d_mixed
    vacc[2:3, :] += column_sum(d_mixed)
    vacc[3:4, :] += column_sum(d_second * normed)
    vacc[4:5, :] += column_sum(d_second)
    vacc[5:6, :] += column_sum(upstream)

    @pl.when(i == pl.num_programs(0) - 1)
    def _():
        for s in range(4):
            cols = slice(s * width, (s + 1) * width)
            gdown[:, cols] = jnp.transpose(gdown[:, cols])

        def take(b, s):
            source, k = (gup, s) if s < 4 else (gdown, s - 4)
            return source[b * block : (b + 1) * block, k * width : (k + 1) * width]

        pack(side[0] == 0, take, mine, theirs)
        vec_out[...] = vacc[...]


def attention_backward(
    side, img, dx2, qkv, att, probs, w, vec, vec_in, dimg, mine_out, theirs_out, grad, vacc
):
    i = pl.program_id(0)
    width = img.shape[-1]

    @pl.when(i == 0)
    def _():
        grad[...] = jnp.zeros_like(grad)
        vacc[...] = jnp.zeros_like(vacc)
        vacc[0:16, :] = vec_in[...]

    gain = vec[0:1, :]
    normed, inverse = norm_stats(img[0].astype(f32))
    first = (normed * gain + vec[1:2, :]).astype(bf16)
    d_mixed = dx2[0]
    d_mixed_b = d_mixed.astype(bf16)
    attended = att[0]
    grad[:, 3 * width : 4 * width] += dot_tn(attended, d_mixed_b)
    d_att = dot_nt(d_mixed_b, w[:, 3 * width : 4 * width]).astype(bf16)
    products = d_att.astype(f32) * attended.astype(f32)
    lane = lax.broadcasted_iota(jnp.int32, (normed.shape[0], 2 * HEAD), 1)
    low = lane < HEAD
    zero = jnp.zeros((), bf16)
    d_q, d_k, d_v = [], [], []
    for p in range(PAIRS):
        cols = slice(2 * HEAD * p, 2 * HEAD * (p + 1))
        q = qkv[0, :, cols]
        k = qkv[0, :, width + 2 * HEAD * p : width + 2 * HEAD * (p + 1)]
        v = qkv[0, :, 2 * width + 2 * HEAD * p : 2 * width + 2 * HEAD * (p + 1)]
        da = d_att[:, cols]
        both = products[:, cols]
        parts = []
        for a in range(2):
            mine = low if a == 0 else jnp.logical_not(low)
            delta = jnp.sum(jnp.where(mine, both, 0.0), -1, keepdims=True)
            pb = probs[0, 2 * p + a]
            d_probs = dot_nt(jnp.where(mine, da, zero), v)
            d_scores = (pb.astype(f32) * (d_probs - delta)).astype(bf16)
            parts.append((dot(d_scores, k), dot_tn(d_scores, q), dot_tn(pb, da)))
        d_q.append(jnp.where(low, parts[0][0], parts[1][0]) * score_scale)
        d_k.append(jnp.where(low, parts[0][1], parts[1][1]))
        d_v.append(jnp.where(low, parts[0][2], parts[1][2]))
    d_query = jnp.concatenate(d_q, axis=-1)
    d_value = jnp.concatenate(d_v, axis=-1)
    d_joined = jnp.concatenate([d_query, jnp.concatenate(d_k, axis=-1), d_value], axis=-1).astype(bf16)
    grad[:, : 3 * width] += dot_tn(first, d_joined)
    d_first = dot_nt(d_joined, w[:, : 3 * width])
    dimg[0] = d_mixed + norm_backward(d_first, normed, inverse, gain)
    vacc[0:1, :] += column_sum(d_first * normed)
    vacc[1:2, :] += column_sum(d_first)
    vacc[6:7, :] += column_sum(d_query)
    vacc[7:8, :] += column_sum(d_value)

    @pl.when(i == pl.num_programs(0) - 1)
    def _():
        source = lax.broadcasted_iota(jnp.int32, (width, width), 0)
        target = lax.broadcasted_iota(jnp.int32, (width, width), 1)
        pair = vacc[0:8, :].astype(bf16)
        mixed = []
        for j in range(2):
            take_q = (source == 2 * target + j).astype(f32).astype(bf16)
            take_v = (source + width == 2 * target + j).astype(f32).astype(bf16)
            mixed.append(dot(pair, take_q)[6:7, :] + dot(pair, take_v)[7:8, :])
        vacc[6:7, :] = mixed[0]
        vacc[7:8, :] = mixed[1]
        grad[:, 4 * width : 4 * width + 128] = jnp.transpose(vacc[...])
        block, n = mine_out.shape[1:]

        def take(b, s):
            return grad[b * block : (b + 1) * block, s * n : (s + 1) * n]

        pack(side[0] == 0, take, mine_out, theirs_out)


def per_image(*dims):
    return pl.BlockSpec((1, *dims), lambda i: (i,) + (0,) * len(dims))


def fixed(*dims):
    return pl.BlockSpec(dims, lambda i: (0,) * len(dims), pipeline_mode=pl.Buffered(1))


def kept(*dims):
    return pl.BlockSpec(dims, lambda i: (0,) * len(dims))


SERIAL = pltpu.CompilerParams(dimension_semantics=("arbitrary",), vmem_limit_bytes=60 << 20)


def swapped(values):
    return lax.ppermute(values, "gz_1", [(0, 1), (1, 0)])


def spread(piece):
    copies = jnp.broadcast_to(piece[None], (64, *piece.shape))
    return lax.all_to_all(copies, CHIPS, 0, 0, tiled=True)


def join(mine, theirs):
    return (mine.astype(f32) + swapped(theirs).astype(f32)).astype(bf16)


def sum_at_chip(half):
    return jnp.sum(lax.all_to_all(half, CHIPS, 0, 0, tiled=True).astype(f32), 0)


def sum_to_owner(own):
    block, n = own.shape
    own = lax.all_to_all(own.reshape(8, block // 8, n), ROW, 0, 0, tiled=True)
    return jnp.transpose(own, (1, 0, 2)).reshape(block // 8, 8 * n)


def cost(time_us, moved):
    return pl.CostEstimate(flops=int(time_us * 1e9), bytes_accessed=moved, transcendentals=0)


def per_device(
    images,
    cotangent,
    counts,
    ln1_gain,
    ln1_bias,
    w_qkv,
    bias_qv,
    w_out,
    b_out,
    ln2_gain,
    ln2_bias,
    w_up,
    b_up,
    w_down,
    b_down,
):
    slots, tokens, width = images.shape
    rows = w_qkv.shape[0]
    hidden = 4 * width
    vectors = jnp.concatenate(
        [
            jnp.stack([ln1_gain, ln1_bias, b_out, ln2_gain, ln2_bias, b_down], axis=1),
            bias_qv.reshape(rows, 2),
            b_up.reshape(rows, 4),
        ],
        axis=1,
    )
    spare = 2048 - 4 * width - vectors.shape[1]
    shard_one = jnp.concatenate([w_qkv, w_out, vectors, jnp.zeros((rows, spare), bf16)], axis=1)
    up_turned = jnp.transpose(w_up.reshape(rows, width, 4), (0, 2, 1)).reshape(rows, hidden)
    shard_two = jnp.concatenate([up_turned, w_down.reshape(rows, hidden)], axis=1)
    pieces = jnp.concatenate([shard_one.reshape(rows, 8, 256), shard_two.reshape(rows, 8, width)], -1)
    pieces = lax.all_to_all(jnp.transpose(pieces, (1, 0, 2)), ROW, 0, 0, tiled=True)
    pieces = pieces.reshape(8 * rows, 256 + width)
    own_one = spread(pieces[:, :256])
    other_one = swapped(own_one)
    own_two = spread(pieces[:, 256:])
    side = lax.axis_index("gz_1").astype(jnp.int32).reshape(1)
    scalar = pl.BlockSpec(memory_space=pltpu.SMEM)
    block = 8 * rows

    x2, qkv, attended, probs, w_one, vec = pl.pallas_call(
        attention_forward,
        grid=(slots,),
        in_specs=[
            scalar,
            per_image(tokens, width),
            fixed(64, block, 256),
            fixed(64, block, 256),
        ],
        out_specs=[
            per_image(tokens, width),
            per_image(tokens, 3 * width),
            per_image(tokens, width),
            per_image(HEADS, tokens, tokens),
            kept(width, hidden),
            kept(16, width),
        ],
        out_shape=[
            jax.ShapeDtypeStruct((slots, tokens, width), f32),
            jax.ShapeDtypeStruct((slots, tokens, 3 * width), bf16),
            jax.ShapeDtypeStruct((slots, tokens, width), bf16),
            jax.ShapeDtypeStruct((slots, HEADS, tokens, tokens), bf16),
            jax.ShapeDtypeStruct((width, hidden), bf16),
            jax.ShapeDtypeStruct((16, width), f32),
        ],
        compiler_params=SERIAL,
        cost_estimate=cost(17, 12 << 20),
        name="attention_forward",
    )(side, images, own_one, other_one)

    own_two, x2 = lax.optimization_barrier((own_two, x2))
    other_two = swapped(own_two)
    output, dx2, mine_two, theirs_two, vec_two = pl.pallas_call(
        feed_forward,
        grid=(slots,),
        in_specs=[
            scalar,
            scalar,
            per_image(tokens, width),
            per_image(tokens, width),
            fixed(64, block, width),
            fixed(64, block, width),
            fixed(16, width),
        ],
        out_specs=[
            per_image(tokens, width),
            per_image(tokens, width),
            kept(64, block, width),
            kept(64, block, width),
            kept(16, width),
        ],
        out_shape=[
            jax.ShapeDtypeStruct((slots, tokens, width), f32),
            jax.ShapeDtypeStruct((slots, tokens, width), f32),
            jax.ShapeDtypeStruct((64, block, width), bf16),
            jax.ShapeDtypeStruct((64, block, width), bf16),
            jax.ShapeDtypeStruct((16, width), f32),
        ],
        scratch_shapes=[
            pltpu.VMEM((width, 2 * hidden), bf16),
            pltpu.VMEM((width, hidden), f32),
            pltpu.VMEM((width, hidden), f32),
            pltpu.VMEM((16, width), f32),
        ],
        compiler_params=SERIAL,
        cost_estimate=cost(34, 16 << 20),
        name="feed_forward",
    )(side, counts, x2, cotangent, own_two, other_two, vec)

    half_two, dx2 = lax.optimization_barrier((join(mine_two, theirs_two), dx2))
    d_images, mine_one, theirs_one = pl.pallas_call(
        attention_backward,
        grid=(slots,),
        in_specs=[
            scalar,
            per_image(tokens, width),
            per_image(tokens, width),
            per_image(tokens, 3 * width),
            per_image(tokens, width),
            per_image(HEADS, tokens, tokens),
            fixed(width, hidden),
            fixed(16, width),
            fixed(16, width),
        ],
        out_specs=[per_image(tokens, width), kept(64, block, 256), kept(64, block, 256)],
        out_shape=[
            jax.ShapeDtypeStruct((slots, tokens, width), f32),
            jax.ShapeDtypeStruct((64, block, 256), bf16),
            jax.ShapeDtypeStruct((64, block, 256), bf16),
        ],
        scratch_shapes=[pltpu.VMEM((width, 2048), f32), pltpu.VMEM((128, width), f32)],
        compiler_params=SERIAL,
        cost_estimate=cost(28, 14 << 20),
        name="attention_backward",
    )(side, images, dx2, qkv, attended, probs, w_one, vec, vec_two)

    two = sum_to_owner(sum_at_chip(half_two))
    one = sum_to_owner(sum_at_chip(join(mine_one, theirs_one)))
    small = one[:, hidden : hidden + 12]
    up = jnp.transpose(two[:, :hidden].reshape(rows, 4, width), (0, 2, 1)).reshape(rows, hidden)
    return (
        output,
        d_images,
        small[:, 0],
        small[:, 1],
        one[:, : 3 * width],
        small[:, 6:8].reshape(-1),
        one[:, 3 * width : hidden],
        small[:, 2],
        small[:, 3],
        small[:, 4],
        up,
        small[:, 8:12].reshape(-1),
        two[:, hidden:].reshape(4 * rows, width),
        small[:, 5],
    )


def solution(mesh):
    torus = Mesh(
        mesh.devices.reshape(mesh.shape["gx"], mesh.shape["gy"], 4, 2), ("gx", "gy", "gz_0", "gz_1")
    )
    whole, flat, table = P(EVERY, None, None), P(EVERY), P(EVERY, None)
    params = (flat, flat, table, flat, table, flat, flat, flat, table, flat, table, flat)
    return jax.shard_map(
        per_device,
        mesh=torus,
        in_specs=(whole, whole, flat, *params),
        out_specs=(whole, whole, *params),
        check_vma=False,
    )
```

```python
import jax
import jax.numpy as jnp
from jax import lax
from jax.experimental import pallas as pl
from jax.experimental.pallas import tpu as pltpu
from jax.sharding import Mesh
from jax.sharding import PartitionSpec as P

HEADS = 6
HEAD = 64
CHUNK = 512
PAIRS = HEADS // 2
CHIPS = ("gx", "gy", "gz_0")
ROW = ("gz_0", "gz_1")
EVERY = ("gx", "gy", "gz_0", "gz_1")
f32 = jnp.float32
bf16 = jnp.bfloat16

epsilon = 1e-06
score_scale = 0.125
root_half = 0.7071067811865476
inv_root_two_pi = 0.3989422804014327


def dot(left, right):
    return jnp.dot(left, right, preferred_element_type=f32)


def dot_nt(left, right):
    return lax.dot_general(left, right, (((1,), (1,)), ((), ())), preferred_element_type=f32)


def dot_tn(left, right):
    return lax.dot_general(left, right, (((0,), (0,)), ((), ())), preferred_element_type=f32)


def norm_stats(values):
    center = values - jnp.mean(values, -1, keepdims=True)
    inverse = lax.rsqrt(jnp.mean(center * center, -1, keepdims=True) + epsilon)
    return center * inverse, inverse


def norm_backward(upstream, normed, inverse, gain):
    scaled = upstream * gain
    return inverse * (
        scaled
        - jnp.mean(scaled, -1, keepdims=True)
        - normed * jnp.mean(scaled * normed, -1, keepdims=True)
    )


def column_sum(values):
    return jnp.sum(values, 0, keepdims=True)


def unpack(low, own, other, put):
    for b in range(16):
        for x in range(4):
            mine, theirs = own[4 * b + x], other[4 * b + x]
            put(b, 2 * x, jnp.where(low, mine, theirs))
            put(b, 2 * x + 1, jnp.where(low, theirs, mine))


def pack(low, take, mine, theirs):
    for b in range(16):
        for x in range(4):
            even, odd = take(b, 2 * x).astype(bf16), take(b, 2 * x + 1).astype(bf16)
            mine[4 * b + x] = jnp.where(low, even, odd)
            theirs[4 * b + x] = jnp.where(low, odd, even)


def attention_forward(side, img, own, other, x2_out, qkv_out, att_out, probs_out, scale_out, w, vec, turn):
    width = img.shape[-1]
    block, n = own.shape[1:]

    @pl.when(pl.program_id(0) == 0)
    def _():
        tables = []

        def put(b, s, piece):
            if (s + 1) * n <= 4 * width:
                w[b * block : (b + 1) * block, s * n : (s + 1) * n] = piece
            elif s * n == 4 * width:
                tables.append(piece[:, :128].astype(f32))

        unpack(side[0] == 0, own, other, put)
        table = jnp.concatenate(tables, axis=0)
        vec[...] = jnp.transpose(table)[:16, :]
        for first, count, at in ((6, 2, 6), (8, 4, 8)):
            for k in range(count):
                column = jnp.broadcast_to(table[:, first + k : first + k + 1], table.shape)
                turn[pl.ds(k, width, stride=count), :] = column
            for k in range(count):
                vec[at + k : at + k + 1, :] = jnp.transpose(turn[k * width : (k + 1) * width, :])[:1]

    inputs = img[0].astype(f32)
    normed, _ = norm_stats(inputs)
    first = (normed * vec[0:1, :] + vec[1:2, :]).astype(bf16)
    joined = dot(first, w[:, : 3 * width])
    query = ((joined[:, :width] + vec[6:7, :]) * score_scale).astype(bf16)
    keys = joined[:, width : 2 * width].astype(bf16)
    value = (joined[:, 2 * width :] + vec[7:8, :]).astype(bf16)
    qkv_out[0, :, :width] = query
    qkv_out[0, :, width : 2 * width] = keys
    qkv_out[0, :, 2 * width :] = value
    lane = lax.broadcasted_iota(jnp.int32, (inputs.shape[0], 2 * HEAD), 1)
    low = lane < HEAD
    zero = jnp.zeros((), bf16)
    ones = jnp.ones((inputs.shape[0], 2 * HEAD), bf16)
    joined_heads = []
    for p in range(PAIRS):
        cols = slice(2 * HEAD * p, 2 * HEAD * (p + 1))
        q, k = query[:, cols], keys[:, cols]
        extended = jnp.concatenate([value[:, cols], ones], axis=-1)
        outs = []
        for a in range(2):
            masked = jnp.where(low if a == 0 else jnp.logical_not(low), q, zero)
            scores = dot_nt(masked, k)
            raised = jnp.exp(scores - jnp.max(scores, -1, keepdims=True)).astype(bf16)
            probs_out[0, 2 * p + a] = raised
            outs.append(dot(raised, extended))
        weighted = jnp.where(low, outs[0][:, : 2 * HEAD], outs[1][:, : 2 * HEAD])
        scale = 1.0 / jnp.where(low, outs[0][:, 2 * HEAD :], outs[1][:, 2 * HEAD :])
        scale_out[0, :, cols] = scale
        joined_heads.append((weighted * scale).astype(bf16))
    attended = jnp.concatenate(joined_heads, axis=-1)
    att_out[0] = attended
    x2_out[0] = inputs + dot(attended, w[:, 3 * width : 4 * width]) + vec[2:3, :]


def feed_forward(
    side,
    counts,
    x2,
    cot,
    own,
    other,
    vec,
    out,
    dx2_out,
    mine,
    theirs,
    vec_out,
    up,
    down,
    wide,
    gup,
    gdown,
    vacc,
):
    i = pl.program_id(0)
    width = x2.shape[-1]
    hidden = 4 * width
    block = own.shape[1]

    @pl.when(i == 0)
    def _():
        def put(b, s, piece):
            if s < 4:
                up[b * block : (b + 1) * block, s * width : (s + 1) * width] = piece
            else:
                rows = pl.ds(4 * block * b + s - 4, block, stride=4)
                for k in range(width // 128):
                    wide[k, rows, :] = piece[:, 128 * k : 128 * (k + 1)].astype(f32)

        for s in range(3):
            vacc[s * 16 : (s + 1) * 16, :] = jnp.zeros((16, width), f32)
        unpack(side[0] == 0, own, other, put)
        for k in range(width // 128):
            down[:, 128 * k : 128 * (k + 1)] = wide[k].astype(bf16)
        gup[...] = jnp.zeros_like(gup)
        gdown[...] = jnp.zeros_like(gdown)

    mixed = x2[0]
    normed, inverse = norm_stats(mixed)
    gain = vec[3:4, :]
    second = (normed * gain + vec[4:5, :]).astype(bf16)
    live = (i < counts[0]).astype(f32)
    upstream = cot[0].astype(f32) * live
    upstream_b = upstream.astype(bf16)
    bias = jnp.concatenate([vec[8 + s : 9 + s, :] for s in range(4)], axis=-1)
    total = mixed + vec[5:6, :]
    d_second = jnp.zeros_like(mixed)
    sums = []
    for s in range(hidden // CHUNK):
        cols = slice(s * CHUNK, (s + 1) * CHUNK)
        before = dot(second, up[:, cols]) + bias[:, cols]
        cdf = 0.5 * (1.0 + lax.erf(before * root_half))
        active = (before * cdf).astype(bf16)
        slope = cdf + before * jnp.exp(-0.5 * before * before) * inv_root_two_pi
        total = total + dot(active, down[cols, :])
        d_before = dot_nt(upstream_b, down[cols, :]) * slope
        sums.append(column_sum(d_before))
        d_before_b = d_before.astype(bf16)
        gdown[:, cols] += dot_tn(upstream_b, active)
        gup[:, cols] += dot_tn(second, d_before_b)
        d_second = d_second + dot_nt(d_before_b, up[:, cols])
    out[0] = total
    d_mixed = upstream + norm_backward(d_second, normed, inverse, gain)
    dx2_out[0] = d_mixed
    summed = jnp.concatenate(sums, axis=-1)
    for s in range(4):
        vacc[8 + s : 9 + s, :] += summed[:, s * width : (s + 1) * width]
    vacc[2:3, :] += column_sum(d_mixed)
    vacc[3:4, :] += column_sum(d_second * normed)
    vacc[4:5, :] += column_sum(d_second)
    vacc[5:6, :] += column_sum(upstream)

    @pl.when(i == pl.num_programs(0) - 1)
    def _():
        for s in range(4):
            rows = slice(s * width, (s + 1) * width)
            turned = jnp.transpose(gdown[:, rows])
            for k in range(width // 128):
                wide[k, rows, :] = turned[:, 128 * k : 128 * (k + 1)]

        def take(b, s):
            if s < 4:
                return gup[b * block : (b + 1) * block, s * width : (s + 1) * width]
            rows = pl.ds(4 * block * b + s - 4, block, stride=4)
            return jnp.concatenate([wide[k, rows, :] for k in range(width // 128)], axis=-1)

        pack(side[0] == 0, take, mine, theirs)
        vec_out[...] = vacc[0:16, :]


def attention_backward(
    side, img, dx2, qkv, att, probs, scale, w, vec, vec_in, dimg, mine_out, theirs_out, grad, vacc, turn
):
    i = pl.program_id(0)
    width = img.shape[-1]

    @pl.when(i == 0)
    def _():
        grad[...] = jnp.zeros_like(grad)
        vacc[...] = jnp.zeros_like(vacc)
        vacc[0:16, :] = vec_in[...]

    gain = vec[0:1, :]
    normed, inverse = norm_stats(img[0].astype(f32))
    first = (normed * gain + vec[1:2, :]).astype(bf16)
    d_mixed = dx2[0]
    d_mixed_b = d_mixed.astype(bf16)
    attended = att[0]
    grad[:, 3 * width : 4 * width] += dot_tn(attended, d_mixed_b)
    d_att = (dot_nt(d_mixed_b, w[:, 3 * width : 4 * width]) * scale[0]).astype(bf16)
    products = d_att.astype(f32) * attended.astype(f32)
    lane = lax.broadcasted_iota(jnp.int32, (normed.shape[0], 2 * HEAD), 1)
    low = lane < HEAD
    zero = jnp.zeros((), bf16)
    d_q, d_k, d_v = [], [], []
    for p in range(PAIRS):
        cols = slice(2 * HEAD * p, 2 * HEAD * (p + 1))
        q = qkv[0, :, cols]
        k = qkv[0, :, width + 2 * HEAD * p : width + 2 * HEAD * (p + 1)]
        v = qkv[0, :, 2 * width + 2 * HEAD * p : 2 * width + 2 * HEAD * (p + 1)]
        da = d_att[:, cols]
        both = products[:, cols]
        parts = []
        for a in range(2):
            mine = low if a == 0 else jnp.logical_not(low)
            delta = jnp.sum(jnp.where(mine, both, 0.0), -1, keepdims=True)
            pb = probs[0, 2 * p + a]
            d_probs = dot_nt(jnp.where(mine, da, zero), v)
            d_scores = (pb.astype(f32) * (d_probs - delta)).astype(bf16)
            parts.append((dot(d_scores, k), dot_tn(d_scores, q), dot_tn(pb, da)))
        d_q.append(jnp.where(low, parts[0][0], parts[1][0]) * score_scale)
        d_k.append(jnp.where(low, parts[0][1], parts[1][1]))
        d_v.append(jnp.where(low, parts[0][2], parts[1][2]))
    d_query = jnp.concatenate(d_q, axis=-1)
    d_value = jnp.concatenate(d_v, axis=-1)
    d_joined = jnp.concatenate([d_query, jnp.concatenate(d_k, axis=-1), d_value], axis=-1).astype(bf16)
    grad[:, : 3 * width] += dot_tn(first, d_joined)
    d_first = dot_nt(d_joined, w[:, : 3 * width])
    dimg[0] = d_mixed + norm_backward(d_first, normed, inverse, gain)
    vacc[0:1, :] += column_sum(d_first * normed)
    vacc[1:2, :] += column_sum(d_first)
    vacc[6:7, :] += column_sum(d_query)
    vacc[7:8, :] += column_sum(d_value)

    @pl.when(i == pl.num_programs(0) - 1)
    def _():
        table = jnp.transpose(vacc[...])
        place = lax.broadcasted_iota(jnp.int32, table.shape, 1)
        for first, count in ((6, 2), (8, 4)):
            for k in range(count):
                column = table[:, first + k : first + k + 1]
                turn[k * width : (k + 1) * width, :] = jnp.broadcast_to(column, table.shape)
            for k in range(count):
                picked = turn[pl.ds(k, width, stride=count), :]
                table = jnp.where(place == first + k, picked, table)
        grad[:, 4 * width : 4 * width + 128] = table
        block, n = mine_out.shape[1:]

        def take(b, s):
            return grad[b * block : (b + 1) * block, s * n : (s + 1) * n]

        pack(side[0] == 0, take, mine_out, theirs_out)


def per_image(*dims):
    return pl.BlockSpec((1, *dims), lambda i: (i,) + (0,) * len(dims))


def fixed(*dims):
    return pl.BlockSpec(dims, lambda i: (0,) * len(dims), pipeline_mode=pl.Buffered(1))


def kept(*dims):
    return pl.BlockSpec(dims, lambda i: (0,) * len(dims))


SERIAL = pltpu.CompilerParams(dimension_semantics=("arbitrary",), vmem_limit_bytes=60 << 20)


def swapped(values):
    return lax.ppermute(values, "gz_1", [(0, 1), (1, 0)])


def spread(piece):
    copies = jnp.broadcast_to(piece[None], (64, *piece.shape))
    return lax.all_to_all(copies, CHIPS, 0, 0, tiled=True)


def join(mine, theirs):
    return (mine.astype(f32) + swapped(theirs).astype(f32)).astype(bf16)


def sum_at_chip(half):
    return jnp.sum(lax.all_to_all(half, CHIPS, 0, 0, tiled=True).astype(f32), 0)


def pack_shards(vectors, w_qkv, w_out, w_up, w_down, out):
    rows, width = w_qkv.shape[0], w_out.shape[1]
    lanes = vectors.shape[1]
    source = lax.broadcasted_iota(jnp.int32, (lanes, lanes), 0)
    target = lax.broadcasted_iota(jnp.int32, (lanes, lanes), 1)
    line = jnp.broadcast_to(vectors[...], (16, lanes))
    small = []
    for r in range(rows):
        wanted = jnp.where(
            target < 6,
            rows * target + r,
            jnp.where(target < 8, 6 * rows + 2 * r + target - 6, 8 * rows + 4 * r + target - 8),
        )
        chosen = jnp.logical_and(source == wanted, target < 12)
        small.append(dot(line, chosen.astype(f32).astype(bf16))[:1])
    small = jnp.concatenate(small, axis=0).astype(bf16)
    empty = jnp.zeros((rows, 2048 - 4 * width - lanes), bf16)
    first = jnp.concatenate([w_qkv[...], w_out[...], small, empty], axis=-1)
    lower = w_down[...].astype(f32)
    for s in range(8):
        out[s, :, :256] = first[:, 256 * s : 256 * (s + 1)]
        if s < 4:
            out[s, :, 256:] = w_up[:, s * width : (s + 1) * width]
        else:
            picked = [lower[4 * r + s - 4 : 4 * r + s - 3] for r in range(rows)]
            out[s, :, 256:] = jnp.concatenate(picked, axis=0).astype(bf16)


def finish(own, g_qkv, g_out, g_small, g_up, g_down):
    rows, width = g_out.shape
    first = jnp.concatenate([own[s, :, :256] for s in range(8)], axis=-1)
    g_qkv[...] = first[:, : 3 * width]
    g_out[...] = first[:, 3 * width : 4 * width]
    g_small[...] = first[:, 4 * width : 4 * width + 128]
    for s in range(4):
        g_up[:, s * width : (s + 1) * width] = own[s, :, 256:]
        for r in range(rows):
            g_down[4 * r + s : 4 * r + s + 1, :] = own[4 + s, r : r + 1, 256:]


def cost(time_us, moved):
    return pl.CostEstimate(flops=int(time_us * 1e9), bytes_accessed=moved, transcendentals=0)


def per_device(
    images,
    cotangent,
    counts,
    ln1_gain,
    ln1_bias,
    w_qkv,
    bias_qv,
    w_out,
    b_out,
    ln2_gain,
    ln2_bias,
    w_up,
    b_up,
    w_down,
    b_down,
):
    slots, tokens, width = images.shape
    rows = w_qkv.shape[0]
    hidden = 4 * width
    vectors = jnp.concatenate(
        [ln1_gain, ln1_bias, b_out, ln2_gain, ln2_bias, b_down, bias_qv, b_up]
    )
    vectors = jnp.pad(vectors, (0, 128 - vectors.shape[0])).reshape(1, 128)
    pieces = pl.pallas_call(
        pack_shards,
        out_shape=jax.ShapeDtypeStruct((8, rows, 256 + width), bf16),
        name="pack_shards",
    )(vectors, w_qkv, w_out, w_up, w_down)
    pieces = lax.all_to_all(pieces, ROW, 0, 0, tiled=True)
    pieces = pieces.reshape(8 * rows, 256 + width)
    own_one = spread(pieces[:, :256])
    other_one = swapped(own_one)
    own_two = spread(pieces[:, 256:])
    side = lax.axis_index("gz_1").astype(jnp.int32).reshape(1)
    scalar = pl.BlockSpec(memory_space=pltpu.SMEM)
    block = 8 * rows

    x2, qkv, attended, probs, scale, w_one, vec = pl.pallas_call(
        attention_forward,
        grid=(slots,),
        in_specs=[
            scalar,
            per_image(tokens, width),
            fixed(64, block, 256),
            fixed(64, block, 256),
        ],
        out_specs=[
            per_image(tokens, width),
            per_image(tokens, 3 * width),
            per_image(tokens, width),
            per_image(HEADS, tokens, tokens),
            per_image(tokens, width),
            kept(width, hidden),
            kept(16, width),
        ],
        out_shape=[
            jax.ShapeDtypeStruct((slots, tokens, width), f32),
            jax.ShapeDtypeStruct((slots, tokens, 3 * width), bf16),
            jax.ShapeDtypeStruct((slots, tokens, width), bf16),
            jax.ShapeDtypeStruct((slots, HEADS, tokens, tokens), bf16),
            jax.ShapeDtypeStruct((slots, tokens, width), f32),
            jax.ShapeDtypeStruct((width, hidden), bf16),
            jax.ShapeDtypeStruct((16, width), f32),
        ],
        scratch_shapes=[pltpu.VMEM((hidden, 128), f32)],
        compiler_params=SERIAL,
        cost_estimate=cost(17, 12 << 20),
        name="attention_forward",
    )(side, images, own_one, other_one)

    own_two, x2 = lax.optimization_barrier((own_two, x2))
    other_two = swapped(own_two)
    output, dx2, mine_two, theirs_two, vec_two = pl.pallas_call(
        feed_forward,
        grid=(slots,),
        in_specs=[
            scalar,
            scalar,
            per_image(tokens, width),
            per_image(tokens, width),
            fixed(64, block, width),
            fixed(64, block, width),
            fixed(16, width),
        ],
        out_specs=[
            per_image(tokens, width),
            per_image(tokens, width),
            kept(64, block, width),
            kept(64, block, width),
            kept(16, width),
        ],
        out_shape=[
            jax.ShapeDtypeStruct((slots, tokens, width), f32),
            jax.ShapeDtypeStruct((slots, tokens, width), f32),
            jax.ShapeDtypeStruct((64, block, width), bf16),
            jax.ShapeDtypeStruct((64, block, width), bf16),
            jax.ShapeDtypeStruct((16, width), f32),
        ],
        scratch_shapes=[
            pltpu.VMEM((width, hidden), bf16),
            pltpu.VMEM((hidden, width), bf16),
            pltpu.VMEM((width // 128, hidden, 128), f32),
            pltpu.VMEM((width, hidden), f32),
            pltpu.VMEM((width, hidden), f32),
            pltpu.VMEM((48, width), f32),
        ],
        compiler_params=SERIAL,
        cost_estimate=cost(34, 16 << 20),
        name="feed_forward",
    )(side, counts, x2, cotangent, own_two, other_two, vec)

    half_two, dx2 = lax.optimization_barrier((join(mine_two, theirs_two), dx2))
    d_images, mine_one, theirs_one = pl.pallas_call(
        attention_backward,
        grid=(slots,),
        in_specs=[
            scalar,
            per_image(tokens, width),
            per_image(tokens, width),
            per_image(tokens, 3 * width),
            per_image(tokens, width),
            per_image(HEADS, tokens, tokens),
            per_image(tokens, width),
            fixed(width, hidden),
            fixed(16, width),
            fixed(16, width),
        ],
        out_specs=[per_image(tokens, width), kept(64, block, 256), kept(64, block, 256)],
        out_shape=[
            jax.ShapeDtypeStruct((slots, tokens, width), f32),
            jax.ShapeDtypeStruct((64, block, 256), bf16),
            jax.ShapeDtypeStruct((64, block, 256), bf16),
        ],
        scratch_shapes=[
            pltpu.VMEM((width, 2048), f32),
            pltpu.VMEM((128, width), f32),
            pltpu.VMEM((hidden, 128), f32),
        ],
        compiler_params=SERIAL,
        cost_estimate=cost(28, 14 << 20),
        name="attention_backward",
    )(side, images, dx2, qkv, attended, probs, scale, w_one, vec, vec_two)

    sums_two = sum_at_chip(half_two)
    sums_one = sum_at_chip(join(mine_one, theirs_one))
    sums = jnp.concatenate([sums_one, sums_two], axis=-1).reshape(8, rows, 256 + width)
    sums, output, d_images = lax.optimization_barrier(
        (sums, jnp.transpose(output, (1, 0, 2)), jnp.transpose(d_images, (1, 0, 2)))
    )
    output, d_images = jnp.transpose(output, (1, 0, 2)), jnp.transpose(d_images, (1, 0, 2))
    own = lax.all_to_all(sums, ROW, 0, 0, tiled=True)
    g_qkv, g_out, small, g_up, g_down = pl.pallas_call(
        finish,
        out_shape=[
            jax.ShapeDtypeStruct((rows, 3 * width), f32),
            jax.ShapeDtypeStruct((rows, width), f32),
            jax.ShapeDtypeStruct((rows, 128), f32),
            jax.ShapeDtypeStruct((rows, hidden), f32),
            jax.ShapeDtypeStruct((4 * rows, width), f32),
        ],
        name="finish",
    )(own)
    return (
        output,
        d_images,
        small[:, 0],
        small[:, 1],
        g_qkv,
        small[:, 6:8].reshape(-1),
        g_out,
        small[:, 2],
        small[:, 3],
        small[:, 4],
        g_up,
        small[:, 8:12].reshape(-1),
        g_down,
        small[:, 5],
    )


def solution(mesh):
    torus = Mesh(
        mesh.devices.reshape(mesh.shape["gx"], mesh.shape["gy"], 4, 2), ("gx", "gy", "gz_0", "gz_1")
    )
    whole, flat, table = P(EVERY, None, None), P(EVERY), P(EVERY, None)
    params = (flat, flat, table, flat, table, flat, flat, flat, table, flat, table, flat)
    return jax.shard_map(
        per_device,
        mesh=torus,
        in_specs=(whole, whole, flat, *params),
        out_specs=(whole, whole, *params),
        check_vma=False,
    )
```

```python
import jax
import jax.numpy as jnp
from jax import lax
from jax.experimental import pallas as pl
from jax.experimental.pallas import tpu as pltpu
from jax.experimental.layout import Layout, with_layout_constraint
from jax.sharding import Mesh
from jax.sharding import PartitionSpec as P

HEADS = 6
HEAD = 64
CHUNK = 512
PAIRS = HEADS // 2
CHIPS = ("gx", "gy", "gz_0")
ROW = ("gz_0", "gz_1")
EVERY = ("gx", "gy", "gz_0", "gz_1")
f32 = jnp.float32
bf16 = jnp.bfloat16

epsilon = 1e-06
score_scale = 0.125
root_half = 0.7071067811865476
inv_root_two_pi = 0.3989422804014327


def dot(left, right):
    return jnp.dot(left, right, preferred_element_type=f32)


def dot_nt(left, right):
    return lax.dot_general(left, right, (((1,), (1,)), ((), ())), preferred_element_type=f32)


def dot_tn(left, right):
    return lax.dot_general(left, right, (((0,), (0,)), ((), ())), preferred_element_type=f32)


def norm_stats(values):
    center = values - jnp.mean(values, -1, keepdims=True)
    inverse = lax.rsqrt(jnp.mean(center * center, -1, keepdims=True) + epsilon)
    return center * inverse, inverse


def norm_backward(upstream, normed, inverse, gain):
    scaled = upstream * gain
    return inverse * (
        scaled
        - jnp.mean(scaled, -1, keepdims=True)
        - normed * jnp.mean(scaled * normed, -1, keepdims=True)
    )


def column_sum(values):
    return jnp.sum(values, 0, keepdims=True)


def unpack(low, own, other, put):
    for b in range(16):
        for x in range(4):
            mine, theirs = own[4 * b + x], other[4 * b + x]
            put(b, 2 * x, jnp.where(low, mine, theirs))
            put(b, 2 * x + 1, jnp.where(low, theirs, mine))


def pack(low, take, mine, theirs):
    for b in range(16):
        for x in range(4):
            even, odd = take(b, 2 * x).astype(bf16), take(b, 2 * x + 1).astype(bf16)
            mine[4 * b + x] = jnp.where(low, even, odd)
            theirs[4 * b + x] = jnp.where(low, odd, even)


def attention_forward(side, img, own, other, x2_out, qkv_out, att_out, probs_out, scale_out, w, vec, turn):
    width = img.shape[-1]
    block, n = own.shape[1:]

    @pl.when(pl.program_id(0) == 0)
    def _():
        tables = []

        def put(b, s, piece):
            if (s + 1) * n <= 4 * width:
                w[b * block : (b + 1) * block, s * n : (s + 1) * n] = piece
            elif s * n == 4 * width:
                tables.append(piece[:, :128].astype(f32))

        unpack(side[0] == 0, own, other, put)
        table = jnp.concatenate(tables, axis=0)
        vec[...] = jnp.transpose(table)[:16, :]
        for first, count, at in ((6, 2, 6), (8, 4, 8)):
            for k in range(count):
                column = jnp.broadcast_to(table[:, first + k : first + k + 1], table.shape)
                turn[pl.ds(k, width, stride=count), :] = column
            for k in range(count):
                vec[at + k : at + k + 1, :] = jnp.transpose(turn[k * width : (k + 1) * width, :])[:1]

    inputs = img[0].astype(f32)
    normed, _ = norm_stats(inputs)
    first = (normed * vec[0:1, :] + vec[1:2, :]).astype(bf16)
    joined = dot(first, w[:, : 3 * width])
    query = ((joined[:, :width] + vec[6:7, :]) * score_scale).astype(bf16)
    keys = joined[:, width : 2 * width].astype(bf16)
    value = (joined[:, 2 * width :] + vec[7:8, :]).astype(bf16)
    qkv_out[0, :, :width] = query
    qkv_out[0, :, width : 2 * width] = keys
    qkv_out[0, :, 2 * width :] = value
    lane = lax.broadcasted_iota(jnp.int32, (inputs.shape[0], 2 * HEAD), 1)
    low = lane < HEAD
    zero = jnp.zeros((), bf16)
    ones = jnp.ones((inputs.shape[0], 2 * HEAD), bf16)
    joined_heads = []
    for p in range(PAIRS):
        cols = slice(2 * HEAD * p, 2 * HEAD * (p + 1))
        q, k = query[:, cols], keys[:, cols]
        extended = jnp.concatenate([value[:, cols], ones], axis=-1)
        outs = []
        for a in range(2):
            masked = jnp.where(low if a == 0 else jnp.logical_not(low), q, zero)
            scores = dot_nt(masked, k)
            raised = jnp.exp(scores - jnp.max(scores, -1, keepdims=True)).astype(bf16)
            probs_out[0, 2 * p + a] = raised
            outs.append(dot(raised, extended))
        weighted = jnp.where(low, outs[0][:, : 2 * HEAD], outs[1][:, : 2 * HEAD])
        scale = 1.0 / jnp.where(low, outs[0][:, 2 * HEAD :], outs[1][:, 2 * HEAD :])
        scale_out[0, :, cols] = scale
        joined_heads.append((weighted * scale).astype(bf16))
    attended = jnp.concatenate(joined_heads, axis=-1)
    att_out[0] = attended
    x2_out[0] = inputs + dot(attended, w[:, 3 * width : 4 * width]) + vec[2:3, :]


def feed_forward(
    side,
    counts,
    x2,
    cot,
    own,
    other,
    vec,
    out,
    dx2_out,
    mine,
    theirs,
    vec_out,
    up,
    down,
    wide,
    gup,
    gdown,
    vacc,
):
    i = pl.program_id(0)
    width = x2.shape[-1]
    hidden = 4 * width
    block = own.shape[1]

    @pl.when(i == 0)
    def _():
        def put(b, s, piece):
            if s < 4:
                up[b * block : (b + 1) * block, s * width : (s + 1) * width] = piece
            else:
                rows = pl.ds(4 * block * b + s - 4, block, stride=4)
                for k in range(width // 128):
                    wide[k, rows, :] = piece[:, 128 * k : 128 * (k + 1)].astype(f32)

        for s in range(3):
            vacc[s * 16 : (s + 1) * 16, :] = jnp.zeros((16, width), f32)
        unpack(side[0] == 0, own, other, put)
        for k in range(width // 128):
            down[:, 128 * k : 128 * (k + 1)] = wide[k].astype(bf16)
        gup[...] = jnp.zeros_like(gup)
        gdown[...] = jnp.zeros_like(gdown)

    mixed = x2[0]
    normed, inverse = norm_stats(mixed)
    gain = vec[3:4, :]
    second = (normed * gain + vec[4:5, :]).astype(bf16)
    live = (i < counts[0]).astype(f32)
    upstream = cot[0].astype(f32) * live
    upstream_b = upstream.astype(bf16)
    bias = jnp.concatenate([vec[8 + s : 9 + s, :] for s in range(4)], axis=-1)
    total = mixed + vec[5:6, :]
    d_second = jnp.zeros_like(mixed)
    sums = []
    for s in range(hidden // CHUNK):
        cols = slice(s * CHUNK, (s + 1) * CHUNK)
        before = dot(second, up[:, cols]) + bias[:, cols]
        cdf = 0.5 * (1.0 + lax.erf(before * root_half))
        active = (before * cdf).astype(bf16)
        slope = cdf + before * jnp.exp(-0.5 * before * before) * inv_root_two_pi
        total = total + dot(active, down[cols, :])
        d_before = dot_nt(upstream_b, down[cols, :]) * slope
        sums.append(column_sum(d_before))
        d_before_b = d_before.astype(bf16)
        gdown[:, cols] += dot_tn(upstream_b, active)
        gup[:, cols] += dot_tn(second, d_before_b)
        d_second = d_second + dot_nt(d_before_b, up[:, cols])
    out[0] = total
    d_mixed = upstream + norm_backward(d_second, normed, inverse, gain)
    dx2_out[0] = d_mixed
    summed = jnp.concatenate(sums, axis=-1)
    for s in range(4):
        vacc[8 + s : 9 + s, :] += summed[:, s * width : (s + 1) * width]
    vacc[2:3, :] += column_sum(d_mixed)
    vacc[3:4, :] += column_sum(d_second * normed)
    vacc[4:5, :] += column_sum(d_second)
    vacc[5:6, :] += column_sum(upstream)

    @pl.when(i == pl.num_programs(0) - 1)
    def _():
        for s in range(4):
            rows = slice(s * width, (s + 1) * width)
            turned = jnp.transpose(gdown[:, rows])
            for k in range(width // 128):
                wide[k, rows, :] = turned[:, 128 * k : 128 * (k + 1)]

        def take(b, s):
            if s < 4:
                return gup[b * block : (b + 1) * block, s * width : (s + 1) * width]
            rows = pl.ds(4 * block * b + s - 4, block, stride=4)
            return jnp.concatenate([wide[k, rows, :] for k in range(width // 128)], axis=-1)

        pack(side[0] == 0, take, mine, theirs)
        vec_out[...] = vacc[0:16, :]


def attention_backward(
    side, img, dx2, qkv, att, probs, scale, w, vec, vec_in, dimg, mine_out, theirs_out, grad, vacc, turn
):
    i = pl.program_id(0)
    width = img.shape[-1]

    @pl.when(i == 0)
    def _():
        grad[...] = jnp.zeros_like(grad)
        vacc[...] = jnp.zeros_like(vacc)
        vacc[0:16, :] = vec_in[...]

    gain = vec[0:1, :]
    normed, inverse = norm_stats(img[0].astype(f32))
    first = (normed * gain + vec[1:2, :]).astype(bf16)
    d_mixed = dx2[0]
    d_mixed_b = d_mixed.astype(bf16)
    attended = att[0]
    grad[:, 3 * width : 4 * width] += dot_tn(attended, d_mixed_b)
    d_att = (dot_nt(d_mixed_b, w[:, 3 * width : 4 * width]) * scale[0]).astype(bf16)
    products = d_att.astype(f32) * attended.astype(f32)
    lane = lax.broadcasted_iota(jnp.int32, (normed.shape[0], 2 * HEAD), 1)
    low = lane < HEAD
    zero = jnp.zeros((), bf16)
    d_q, d_k, d_v = [], [], []
    for p in range(PAIRS):
        cols = slice(2 * HEAD * p, 2 * HEAD * (p + 1))
        q = qkv[0, :, cols]
        k = qkv[0, :, width + 2 * HEAD * p : width + 2 * HEAD * (p + 1)]
        v = qkv[0, :, 2 * width + 2 * HEAD * p : 2 * width + 2 * HEAD * (p + 1)]
        da = d_att[:, cols]
        both = products[:, cols]
        parts = []
        for a in range(2):
            mine = low if a == 0 else jnp.logical_not(low)
            delta = jnp.sum(jnp.where(mine, both, 0.0), -1, keepdims=True)
            pb = probs[0, 2 * p + a]
            d_probs = dot_nt(jnp.where(mine, da, zero), v)
            d_scores = (pb.astype(f32) * (d_probs - delta)).astype(bf16)
            parts.append((dot(d_scores, k), dot_tn(d_scores, q), dot_tn(pb, da)))
        d_q.append(jnp.where(low, parts[0][0], parts[1][0]) * score_scale)
        d_k.append(jnp.where(low, parts[0][1], parts[1][1]))
        d_v.append(jnp.where(low, parts[0][2], parts[1][2]))
    d_query = jnp.concatenate(d_q, axis=-1)
    d_value = jnp.concatenate(d_v, axis=-1)
    d_joined = jnp.concatenate([d_query, jnp.concatenate(d_k, axis=-1), d_value], axis=-1).astype(bf16)
    grad[:, : 3 * width] += dot_tn(first, d_joined)
    d_first = dot_nt(d_joined, w[:, : 3 * width])
    dimg[0] = d_mixed + norm_backward(d_first, normed, inverse, gain)
    vacc[0:1, :] += column_sum(d_first * normed)
    vacc[1:2, :] += column_sum(d_first)
    vacc[6:7, :] += column_sum(d_query)
    vacc[7:8, :] += column_sum(d_value)

    @pl.when(i == pl.num_programs(0) - 1)
    def _():
        table = jnp.transpose(vacc[...])
        place = lax.broadcasted_iota(jnp.int32, table.shape, 1)
        for first, count in ((6, 2), (8, 4)):
            for k in range(count):
                column = table[:, first + k : first + k + 1]
                turn[k * width : (k + 1) * width, :] = jnp.broadcast_to(column, table.shape)
            for k in range(count):
                picked = turn[pl.ds(k, width, stride=count), :]
                table = jnp.where(place == first + k, picked, table)
        grad[:, 4 * width : 4 * width + 128] = table
        block, n = mine_out.shape[1:]

        def take(b, s):
            return grad[b * block : (b + 1) * block, s * n : (s + 1) * n]

        pack(side[0] == 0, take, mine_out, theirs_out)


def per_image(*dims):
    return pl.BlockSpec((1, *dims), lambda i: (i,) + (0,) * len(dims))


def fixed(*dims):
    return pl.BlockSpec(dims, lambda i: (0,) * len(dims), pipeline_mode=pl.Buffered(1))


def kept(*dims):
    return pl.BlockSpec(dims, lambda i: (0,) * len(dims))


SERIAL = pltpu.CompilerParams(dimension_semantics=("arbitrary",), vmem_limit_bytes=57 << 20)


def swapped(values):
    return lax.ppermute(values, "gz_1", [(0, 1), (1, 0)])


def spread(piece):
    copies = jnp.broadcast_to(piece[None], (64, *piece.shape))
    return lax.all_to_all(copies, CHIPS, 0, 0, tiled=True)


def join(mine, theirs):
    return (mine.astype(f32) + swapped(theirs).astype(f32)).astype(bf16)


def sum_at_chip(half):
    return jnp.sum(lax.all_to_all(half, CHIPS, 0, 0, tiled=True).astype(f32), 0)


def pack_shards(vectors, w_qkv, w_out, w_up, w_down, out):
    rows, width = w_qkv.shape[0], w_out.shape[1]
    lanes = vectors.shape[1]
    source = lax.broadcasted_iota(jnp.int32, (lanes, lanes), 0)
    target = lax.broadcasted_iota(jnp.int32, (lanes, lanes), 1)
    line = jnp.broadcast_to(vectors[...], (16, lanes))
    small = []
    for r in range(rows):
        wanted = jnp.where(
            target < 6,
            rows * target + r,
            jnp.where(target < 8, 6 * rows + 2 * r + target - 6, 8 * rows + 4 * r + target - 8),
        )
        chosen = jnp.logical_and(source == wanted, target < 12)
        small.append(dot(line, chosen.astype(f32).astype(bf16))[:1])
    small = jnp.concatenate(small, axis=0).astype(bf16)
    empty = jnp.zeros((rows, 2048 - 4 * width - lanes), bf16)
    first = jnp.concatenate([w_qkv[...], w_out[...], small, empty], axis=-1)
    lower = w_down[...].astype(f32)
    for s in range(8):
        out[s, :, :256] = first[:, 256 * s : 256 * (s + 1)]
        if s < 4:
            out[s, :, 256:] = w_up[:, s * width : (s + 1) * width]
        else:
            picked = [lower[4 * r + s - 4 : 4 * r + s - 3] for r in range(rows)]
            out[s, :, 256:] = jnp.concatenate(picked, axis=0).astype(bf16)


def finish(own, g_qkv, g_out, g_up, g_down, g_qv, g_bup, *g_rows):
    rows, width = g_out.shape
    first = jnp.concatenate([own[s, :, :256] for s in range(8)], axis=-1)
    g_qkv[...] = first[:, : 3 * width]
    g_out[...] = first[:, 3 * width : 4 * width]
    small = first[:, 4 * width : 4 * width + 128]
    turned = jnp.transpose(jnp.concatenate([small, jnp.zeros((128 - rows, 128), f32)], axis=0))
    for k, g_row in enumerate(g_rows):
        g_row[...] = turned[k : k + 1, :rows]
    source = lax.broadcasted_iota(jnp.int32, (128, 128), 0)
    target = lax.broadcasted_iota(jnp.int32, (128, 128), 1)
    for g_row, lane, count in ((g_qv, 6, 2), (g_bup, 8, 4)):
        line = jnp.zeros((1, 128), f32)
        for r in range(rows):
            held = jnp.logical_and(source >= lane, source < lane + count)
            chosen = jnp.logical_and(held, source - lane + count * r == target)
            line = line + jnp.sum(jnp.where(chosen, turned[:, r : r + 1], 0.0), 0, keepdims=True)
        g_row[...] = line[:, : count * rows]
    for s in range(4):
        g_up[:, s * width : (s + 1) * width] = own[s, :, 256:]
        for r in range(rows):
            g_down[4 * r + s : 4 * r + s + 1, :] = own[4 + s, r : r + 1, 256:]


def held(values):
    return pltpu.with_memory_space_constraint(values, pltpu.VMEM)


def cost(time_us, moved):
    return pl.CostEstimate(flops=int(time_us * 1e9), bytes_accessed=moved, transcendentals=0)


def per_device(
    images,
    cotangent,
    counts,
    ln1_gain,
    ln1_bias,
    w_qkv,
    bias_qv,
    w_out,
    b_out,
    ln2_gain,
    ln2_bias,
    w_up,
    b_up,
    w_down,
    b_down,
):
    slots, tokens, width = images.shape
    rows = w_qkv.shape[0]
    hidden = 4 * width
    vectors, at = jnp.zeros((128,), bf16), 0
    for vector in (ln1_gain, ln1_bias, b_out, ln2_gain, ln2_bias, b_down, bias_qv, b_up):
        length = vector.shape[0]
        vectors = vectors + jnp.pad(vector, (at, 128 - at - length))
        at += length
    vectors = vectors.reshape(1, 128)
    pieces = pl.pallas_call(
        pack_shards,
        out_shape=jax.ShapeDtypeStruct((8, rows, 256 + width), bf16),
        name="pack_shards",
    )(vectors, w_qkv, w_out, w_up, w_down)
    pieces = lax.all_to_all(pieces, ROW, 0, 0, tiled=True)
    pieces = pieces.reshape(8 * rows, 256 + width)
    own_one = spread(pieces[:, :256])
    other_one = swapped(own_one)
    own_two = spread(pieces[:, 256:])
    side = lax.axis_index("gz_1").astype(jnp.int32).reshape(1)
    scalar = pl.BlockSpec(memory_space=pltpu.SMEM)
    resident = pl.BlockSpec(memory_space=pltpu.VMEM)
    block = 8 * rows

    x2, qkv, attended, probs, scale, w_one, vec = pl.pallas_call(
        attention_forward,
        grid=(slots,),
        in_specs=[
            scalar,
            per_image(tokens, width),
            resident,
            resident,
        ],
        out_specs=[
            per_image(tokens, width),
            per_image(tokens, 3 * width),
            per_image(tokens, width),
            per_image(HEADS, tokens, tokens),
            per_image(tokens, width),
            kept(width, hidden),
            kept(16, width),
        ],
        out_shape=[
            jax.ShapeDtypeStruct((slots, tokens, width), f32),
            jax.ShapeDtypeStruct((slots, tokens, 3 * width), bf16),
            jax.ShapeDtypeStruct((slots, tokens, width), bf16),
            jax.ShapeDtypeStruct((slots, HEADS, tokens, tokens), bf16),
            jax.ShapeDtypeStruct((slots, tokens, width), f32),
            jax.ShapeDtypeStruct((width, hidden), bf16),
            jax.ShapeDtypeStruct((16, width), f32),
        ],
        scratch_shapes=[pltpu.VMEM((hidden, 128), f32)],
        compiler_params=SERIAL,
        cost_estimate=cost(17, 12 << 20),
        name="attention_forward",
    )(side, images, *[held(x) for x in (own_one, other_one)])

    own_two, x2 = lax.optimization_barrier((own_two, x2))
    other_two = swapped(own_two)
    output, dx2, mine_two, theirs_two, vec_two = pl.pallas_call(
        feed_forward,
        grid=(slots,),
        in_specs=[
            scalar,
            scalar,
            per_image(tokens, width),
            per_image(tokens, width),
            resident,
            resident,
            fixed(16, width),
        ],
        out_specs=[
            per_image(tokens, width),
            per_image(tokens, width),
            resident,
            resident,
            kept(16, width),
        ],
        out_shape=[
            jax.ShapeDtypeStruct((slots, tokens, width), f32),
            jax.ShapeDtypeStruct((slots, tokens, width), f32),
            pltpu.VMEM((64, block, width), bf16),
            pltpu.VMEM((64, block, width), bf16),
            jax.ShapeDtypeStruct((16, width), f32),
        ],
        scratch_shapes=[
            pltpu.VMEM((width, hidden), bf16),
            pltpu.VMEM((hidden, width), bf16),
            pltpu.VMEM((width // 128, hidden, 128), f32),
            pltpu.VMEM((width, hidden), f32),
            pltpu.VMEM((width, hidden), f32),
            pltpu.VMEM((48, width), f32),
        ],
        compiler_params=SERIAL,
        cost_estimate=cost(34, 16 << 20),
        name="feed_forward",
    )(side, counts, x2, cotangent, held(own_two), held(other_two), vec)

    half_two, dx2 = lax.optimization_barrier((join(mine_two, theirs_two), dx2))
    d_images, mine_one, theirs_one = pl.pallas_call(
        attention_backward,
        grid=(slots,),
        in_specs=[
            scalar,
            per_image(tokens, width),
            per_image(tokens, width),
            per_image(tokens, 3 * width),
            per_image(tokens, width),
            per_image(HEADS, tokens, tokens),
            per_image(tokens, width),
            fixed(width, hidden),
            fixed(16, width),
            fixed(16, width),
        ],
        out_specs=[per_image(tokens, width), resident, resident],
        out_shape=[
            jax.ShapeDtypeStruct((slots, tokens, width), f32),
            pltpu.VMEM((64, block, 256), bf16),
            pltpu.VMEM((64, block, 256), bf16),
        ],
        scratch_shapes=[
            pltpu.VMEM((width, 2048), f32),
            pltpu.VMEM((128, width), f32),
            pltpu.VMEM((hidden, 128), f32),
        ],
        compiler_params=SERIAL,
        cost_estimate=cost(28, 14 << 20),
        name="attention_backward",
    )(side, images, dx2, qkv, attended, probs, scale, w_one, vec, vec_two)

    sums_two = sum_at_chip(half_two)
    sums_one = sum_at_chip(join(mine_one, theirs_one))
    sums = jnp.concatenate([sums_one, sums_two], axis=-1).reshape(8, rows, 256 + width)
    slot_minor = Layout(major_to_minor=(1, 0, 2))
    output = with_layout_constraint(output, slot_minor)
    d_images = with_layout_constraint(d_images, slot_minor)
    sums, output, d_images = lax.optimization_barrier((sums, output, d_images))
    own = lax.all_to_all(sums, ROW, 0, 0, tiled=True)
    g_qkv, g_out, g_up, g_down, g_qv, g_bup, *g_rows = pl.pallas_call(
        finish,
        out_shape=[
            jax.ShapeDtypeStruct((rows, 3 * width), f32),
            jax.ShapeDtypeStruct((rows, width), f32),
            jax.ShapeDtypeStruct((rows, hidden), f32),
            jax.ShapeDtypeStruct((4 * rows, width), f32),
            jax.ShapeDtypeStruct((1, 2 * rows), f32),
            jax.ShapeDtypeStruct((1, 4 * rows), f32),
            *[jax.ShapeDtypeStruct((1, rows), f32)] * 6,
        ],
        name="finish",
    )(own)
    g_gain1, g_bias1, g_bout, g_gain2, g_bias2, g_bdown = [row.reshape(-1) for row in g_rows]
    return (
        output,
        d_images,
        g_gain1,
        g_bias1,
        g_qkv,
        g_qv.reshape(-1),
        g_out,
        g_bout,
        g_gain2,
        g_bias2,
        g_up,
        g_bup.reshape(-1),
        g_down,
        g_bdown,
    )


def solution(mesh):
    torus = Mesh(
        mesh.devices.reshape(mesh.shape["gx"], mesh.shape["gy"], 4, 2), ("gx", "gy", "gz_0", "gz_1")
    )
    whole, flat, table = P(EVERY, None, None), P(EVERY), P(EVERY, None)
    params = (flat, flat, table, flat, table, flat, flat, flat, table, flat, table, flat)
    return jax.shard_map(
        per_device,
        mesh=torus,
        in_specs=(whole, whole, flat, *params),
        out_specs=(whole, whole, *params),
        check_vma=False,
    )
```
